768 devices in a mesh: wave: 96 (over z, x, core), band: 8 (over y).
Axes of the slice: x: 4, y: 8, z: 12, core: 2. Of those that a mesh axis runs over, the one named last changes fastest.
Arguments:
- spectral: bfloat16 [2016, 2, 128, 1280], P('wave', None, 'band'), may hold values from -0.0059814453 to 0.0059814453
- legendre: bfloat16 [2016, 96, 1280], P('wave'), may hold values from -4 to 4
- slot_wave: int32 [2016], replicated, may hold values from 0 to 1280, as said below
- lat_points: int32 [96], P('wave'), may hold values from 20 to 5136, as said below
- level_mix: float32 [32, 32], replicated, may hold values from -1 to 1
- grid_scale: float32 [96, 6144], P('wave', 'band'), may hold values from 0.5 to 2
- gauss_w: float32 [96], replicated, may hold values from 2 to 8
Outputs:
- grid_out: float32 [128, 96, 6144], P(None, 'wave', 'band')
- spec_out: bfloat16 [2016, 2, 128, 1280], P('wave', None, 'band')
The draws below stay inside these ranges and needn't reach their ends.
Inputs may be any that keep to these rules, and one draw needn't show every extreme that they name: `slot_wave`: every wavenumber 0 to 1279 is held by exactly one slot; all other slots hold 1280; some index of wave has all 21 of its slots holding wavenumbers. `lat_points`: each value is 20 + 4 i for a latitude row i from 0 to 1279; some latitude has 5136 points.
All inputs are finite; a program needn't handle non-finite values.
Results may differ from the reference program's by a relative error of at most 0.0062.
Values may be sent and summed in bfloat16 or wider, within the bound.
No kernel may reach another device: no remote copies, remote signals or barrier semaphores. Data moves between devices by JAX's collectives and lax.ppermute only.
A program may use at most 64 MiB of HBM per device.

```python
import math
import jax
import jax.numpy as jnp
from jax import lax

M = 1280
NLEV = 32
FIELDS = 128
LAT = 96
MSLOT = 21
SLOTS = 2016
LONS = 6144


def draw_slot_wave(key, part):
    key_full = jax.random.fold_in(key, 11)
    key_rank = jax.random.fold_in(key, 12)
    key_wave = jax.random.fold_in(key, 13)
    full_device = jax.random.randint(key_full, (), 0, SLOTS // MSLOT)
    slot_index = jnp.arange(SLOTS, dtype=jnp.int32)
    in_full = slot_index // MSLOT == full_device
    random_rank = jax.random.permutation(key_rank, SLOTS).astype(jnp.int32)
    score = jnp.where(in_full, -1, random_rank)
    order = jnp.argsort(score, stable=True).astype(jnp.int32)
    position = jnp.zeros((SLOTS,), jnp.int32).at[order].set(slot_index)
    wave_perm = jax.random.permutation(key_wave, M).astype(jnp.int32)
    live_slot = position < M
    picked = wave_perm[jnp.minimum(position, M - 1)]
    return jnp.where(live_slot, picked, M).astype(jnp.int32)


def draw_lat_points(key, part):
    key_rows = jax.random.fold_in(key, 21)
    key_spot = jax.random.fold_in(key, 22)
    lat_rows = jax.random.randint(key_rows, (LAT,), 0, M)
    spot = jax.random.randint(key_spot, (), 0, LAT)
    lat_rows = jnp.where(jnp.arange(LAT) == spot, M - 1, lat_rows)
    return (20 + 4 * lat_rows).astype(jnp.int32)


def block_levels(rng, extent, cuts, least, largest):
    def one(dim, parts):
        steps = jax.random.uniform(jax.random.fold_in(jax.random.fold_in(rng, 6), dim), (parts,), jnp.float32, least / len(cuts), largest / len(cuts))
        return jnp.repeat(jnp.exp(steps), extent[dim] // parts).reshape((-1,) + (1,) * (len(extent) - dim - 1))

    level = one(*cuts[0])
    for cut in cuts[1:]:
        level = level * one(*cut)
    return level


def gaussian(rng, shape, scale, bound, pieces=(), kind=jnp.bfloat16):
    drawn = jax.random.normal(rng, shape, jnp.float32) * scale
    if len(pieces) > 0:
        drawn = block_levels(rng, shape, pieces, -0.22, 0.18) * drawn
    return jnp.clip(drawn, min=-bound, max=bound).astype(kind)


def setup_inputs(seed: int = 0) -> dict:
    seeds = jax.random.split(jax.random.key(seed), 8)
    spectral = gaussian(seeds[0], (SLOTS, 2, FIELDS, M), 0.001, 0.0059814453, ((0, 96), (2, 8)))
    legendre = gaussian(seeds[1], (SLOTS, LAT, M), 1.0, 4.0, ((0, 96),))
    slot_wave = draw_slot_wave(jax.random.fold_in(seeds[7], 71), 0)
    lat_points = draw_lat_points(jax.random.fold_in(seeds[7], 71), 0)
    level_mix = gaussian(seeds[4], (NLEV, NLEV), NLEV ** -0.5, 1.0, (), jnp.float32)
    grid_scale = jnp.clip(jnp.exp(math.log(2.0) - 1.3862944 * jax.random.uniform(seeds[5], (LAT, LONS), jnp.float32) ** block_levels(seeds[5], (LAT, LONS), ((0, 96), (1, 8)), -0.2, 0.2)), 0.5, 2.0)
    gauss_w = jnp.clip(jnp.exp(jax.random.uniform(seeds[6], (LAT,), jnp.float32, math.log(2.0), math.log(8.0))), 2.0, 8.0)
    return dict(spectral=spectral, legendre=legendre, slot_wave=slot_wave, lat_points=lat_points, level_mix=level_mix, grid_scale=grid_scale, gauss_w=gauss_w)


TWO_PI = 2.0 * math.pi


def trig_table(wave_ids, points, lon_first, lon_width):
    lon_index = lon_first + jnp.arange(lon_width, dtype=jnp.int32)
    turn_index = (wave_ids[None, :, None] * lon_index[None, None, :]) % points[:, None, None]
    angle_rad = turn_index.astype(jnp.float32) * (TWO_PI / points.astype(jnp.float32))[:, None, None]
    return jnp.stack([jnp.cos(angle_rad), jnp.sin(angle_rad)], axis=2)


def valid_waves(wave_ids, points):
    return ((wave_ids[None, :] < M) & (2 * wave_ids[None, :] < points[:, None])).astype(jnp.float32)


def lon_mask(points, lon_first, lon_width):
    lon_index = lon_first + jnp.arange(lon_width, dtype=jnp.int32)
    return (lon_index[None, :] < points[:, None]).astype(jnp.float32)


def inverse_terms(four_coef, wave_ids, points, lon_first, lon_width):
    valid_wave = valid_waves(wave_ids, points)
    doubled = jnp.where(wave_ids == 0, 1.0, 2.0).astype(jnp.float32)
    sign_pair = jnp.array([1.0, -1.0], jnp.float32)
    factor = (valid_wave * doubled[None, :])[:, :, None] * sign_pair
    weighted = four_coef.astype(jnp.float32) * jnp.transpose(factor, (1, 2, 0))[:, :, None, :]
    trig_tab = trig_table(wave_ids, points, lon_first, lon_width)
    grid_rows = jnp.einsum('scfa,ascj->faj', weighted, trig_tab, precision=lax.Precision.HIGHEST)
    return grid_rows * lon_mask(points, lon_first, lon_width)[None]


def direct_terms(grid_rows, wave_ids, points, lon_first, lon_width):
    valid_wave = valid_waves(wave_ids, points)
    sign_pair = jnp.array([1.0, -1.0], jnp.float32)
    trig_tab = trig_table(wave_ids, points, lon_first, lon_width)
    masked_rows = grid_rows * lon_mask(points, lon_first, lon_width)[None]
    summed = jnp.einsum('faj,ascj->fsca', masked_rows, trig_tab, precision=lax.Precision.HIGHEST)
    factor = valid_wave[:, :, None] * sign_pair / points.astype(jnp.float32)[:, None, None]
    return summed * jnp.transpose(factor, (1, 2, 0))[None]


def mix_levels(grid_rows, level_mix, grid_scale):
    fields, lats, lons = grid_rows.shape
    stacked = grid_rows.reshape(fields // NLEV, NLEV, lats, lons)
    mixed_grid = jnp.einsum('ik,bkaj->biaj', level_mix, stacked, precision=lax.Precision.HIGHEST)
    return mixed_grid.reshape(fields, lats, lons) * grid_scale[None]


def reference(spectral, legendre, slot_wave, lat_points, level_mix, grid_scale, gauss_w):
    degree = jnp.arange(M, dtype=jnp.int32)

    def inverse_slot(item):
        spec_slot, leg_slot, wave_slot = item
        masked = jnp.where(degree >= wave_slot, spec_slot.astype(jnp.float32), 0.0)
        return jnp.einsum('cfn,ln->cfl', masked, leg_slot.astype(jnp.float32)).astype(jnp.bfloat16)

    four_coef = lax.map(inverse_slot, (spectral, legendre, slot_wave))
    slot_of = jnp.zeros((M + 1,), jnp.int32).at[slot_wave].set(jnp.arange(SLOTS, dtype=jnp.int32))[:M]
    by_wave = jnp.take(four_coef, slot_of, axis=0)
    lat_major = jnp.moveaxis(by_wave, 3, 0)

    def per_latitude(item):
        coef_lat, points, scale_row = item
        grid_rows = inverse_terms(coef_lat[..., None], degree, points[None], 0, LONS)
        mixed_grid = mix_levels(grid_rows, level_mix, scale_row[None])
        back_coef = direct_terms(mixed_grid, degree, points[None], 0, LONS)
        return grid_rows[:, 0], back_coef[..., 0]

    grid_lat, back_lat = lax.map(per_latitude, (lat_major, lat_points, grid_scale))
    grid_out = jnp.moveaxis(grid_lat, 0, 1)
    fourier_back = lax.optimization_barrier(back_lat.astype(jnp.bfloat16))
    weighted = (fourier_back.astype(jnp.float32) * gauss_w[:, None, None, None]).astype(jnp.bfloat16)
    by_slot = jnp.take(weighted, jnp.minimum(slot_wave, M - 1), axis=2)

    def direct_slot(item):
        coef_slot, leg_slot, wave_slot = item
        summed = jnp.einsum('lfc,ln->cfn', coef_slot.astype(jnp.float32), leg_slot.astype(jnp.float32))
        return jnp.where(degree >= wave_slot, summed, 0.0).astype(jnp.bfloat16)

    spec_out = lax.map(direct_slot, (jnp.moveaxis(by_slot, 2, 0), legendre, slot_wave))
    return grid_out, spec_out
```

```python
import math

import jax
import jax.numpy as jnp
from jax import lax
from jax.experimental import pallas as pl
from jax.experimental.pallas import tpu as pltpu
from jax.sharding import PartitionSpec as P


M = 1280
LAT = 96
GROUP = 3
ROWS = 8
KPAD = GROUP * LAT * ROWS
QPAD = 1408
LONS = 6144
TWO_PI = 2.0 * math.pi
F32 = jnp.float32
BF16 = jnp.bfloat16

NT = (((1,), (1,)), ((), ()))


def spectral_copies(spec_ref, leg_ref, spec_buf, leg_buf, sems):
    copies = []
    for step in range(leg_ref.shape[0] // GROUP):
        at = pl.ds(step * GROUP, GROUP)
        copies.append(
            (
                pltpu.make_async_copy(spec_ref.at[at], spec_buf.at[at], sems.at[0, step]),
                pltpu.make_async_copy(leg_ref.at[at], leg_buf.at[at], sems.at[1, step]),
            )
        )
    return copies


def legendre_inverse_kernel(base_ref, wave_ref, spec_ref, leg_ref, out_ref, spec_buf, leg_buf, acc_ref, sems):
    copies = spectral_copies(spec_ref, leg_ref, spec_buf, leg_buf, sems)
    for pair in copies:
        for copy in pair:
            copy.start()
    acc_ref[pl.ds(ROWS - 1, LAT, stride=ROWS), :] = jnp.zeros((LAT, 128), F32)
    degree = lax.broadcasted_iota(jnp.int32, (32, M), 1)
    for step, pair in enumerate(copies):
        for copy in pair:
            copy.wait()
        parts = []
        for k in range(step * GROUP, step * GROUP + GROUP):
            wave = wave_ref[base_ref[0] + k]
            coef = jnp.where(degree >= wave, spec_buf[k].astype(F32), 0.0).astype(BF16)
            parts.append(lax.dot_general(leg_buf[k], coef, NT, preferred_element_type=F32))
        parts.append(jnp.zeros((LAT, 32), F32))
        acc_ref[pl.ds(step, LAT, stride=ROWS), :] = jnp.concatenate(parts, axis=1)
    out_ref[...] = acc_ref[...].astype(BF16)


def legendre_inverse(base, slot_wave, spectral, legendre):
    slots = spectral.shape[0]
    smem = pl.BlockSpec(memory_space=pltpu.SMEM)
    hbm = pl.BlockSpec(memory_space=pl.ANY)
    return pl.pallas_call(
        legendre_inverse_kernel,
        in_specs=[smem, smem, hbm, hbm],
        out_specs=pl.BlockSpec(memory_space=pltpu.VMEM),
        out_shape=jax.ShapeDtypeStruct((LAT * ROWS, 128), BF16),
        scratch_shapes=[
            pltpu.VMEM((slots, 32, M), BF16),
            pltpu.VMEM((slots, LAT, M), BF16),
            pltpu.VMEM((LAT * ROWS, 128), F32),
            pltpu.SemaphoreType.DMA((2, slots // GROUP)),
        ],
        name="legendre_inverse",
    )(base, slot_wave, spectral.reshape(slots, 32, M), legendre)


def legendre_direct_kernel(base_ref, wave_ref, coef_ref, leg_ref, gauss_ref, out_ref, leg_buf, out_buf, acc_ref, sems):
    steps = leg_ref.shape[0] // GROUP
    loads = []
    stores = []
    for step in range(steps):
        at = pl.ds(step * GROUP, GROUP)
        loads.append(pltpu.make_async_copy(leg_ref.at[at], leg_buf.at[at], sems.at[0, step]))
        stores.append(pltpu.make_async_copy(out_buf.at[at], out_ref.at[at], sems.at[1, step]))
    for copy in loads:
        copy.start()
    acc_ref[pl.ds(0, LAT * ROWS), :] = coef_ref[...].astype(F32)
    acc_ref[pl.ds(LAT * ROWS, (128 - LAT) * ROWS), :] = jnp.zeros(((128 - LAT) * ROWS, 128), F32)
    degree = lax.broadcasted_iota(jnp.int32, (32, M), 1)
    for step in range(steps):
        rows = acc_ref[pl.ds(step, 128, stride=ROWS), :]
        weighted = (rows.T[:, :LAT] * gauss_ref[...]).astype(BF16)
        loads[step].wait()
        for j in range(GROUP):
            k = step * GROUP + j
            wave = wave_ref[base_ref[0] + k]
            summed = jnp.dot(weighted[32 * j : 32 * j + 32], leg_buf[k], preferred_element_type=F32)
            out_buf[k] = jnp.where(degree >= wave, summed, 0.0).astype(BF16)
        stores[step].start()
    for copy in stores:
        copy.wait()


def legendre_direct(base, slot_wave, coef, legendre, gauss_w):
    slots = legendre.shape[0]
    smem = pl.BlockSpec(memory_space=pltpu.SMEM)
    vmem = pl.BlockSpec(memory_space=pltpu.VMEM)
    hbm = pl.BlockSpec(memory_space=pl.ANY)
    return pl.pallas_call(
        legendre_direct_kernel,
        in_specs=[smem, smem, vmem, hbm, vmem],
        out_specs=hbm,
        out_shape=jax.ShapeDtypeStruct((slots, 32, M), BF16),
        scratch_shapes=[
            pltpu.VMEM((slots, LAT, M), BF16),
            pltpu.VMEM((slots, 32, M), BF16),
            pltpu.VMEM((128 * ROWS, 128), F32),
            pltpu.SemaphoreType.DMA((2, slots // GROUP)),
        ],
        name="legendre_direct",
    )(base, slot_wave, coef, legendre, gauss_w[None, :])


def turn(product, points, inverse, quarter):
    rest = product - jnp.floor(product * inverse) * points
    rest = jnp.where(rest < 0.0, rest + points, rest)
    rest = jnp.where(rest >= points, rest - points, rest)
    quad = jnp.floor(rest * (4.0 * inverse) + 0.5)
    x = (rest - quad * quarter) * (TWO_PI * inverse)
    x2 = x * x
    s = x + x * x2 * (-1.6666654611e-1 + x2 * (8.3321608736e-3 - x2 * 1.9515295891e-4))
    c = 1.0 - 0.5 * x2 + x2 * x2 * (
        4.166664568298827e-2 + x2 * (-1.388731625493765e-3 + x2 * 2.443315711809948e-5)
    )
    swap = (quad == 1.0) | (quad == 3.0)
    cos = jnp.where(swap, s, c)
    sin = jnp.where(swap, c, s)
    cos = jnp.where((quad == 1.0) | (quad == 2.0), -cos, cos)
    sin = jnp.where((quad == 2.0) | (quad == 3.0), -sin, sin)
    return cos, sin


TROWS = 32


def table_kernel(points_ref, wave_ref, cos_ref, sin_ref, row_ref, even_ref, odd_ref):
    points_int = points_ref[0]

    def constants(rows):
        points = jnp.full((rows, 128), points_int, jnp.int32).astype(F32)
        quarter = jnp.full((rows, 128), points_int >> 2, jnp.int32).astype(F32)
        return points, 1.0 / points, quarter

    blocks = wave_ref.shape[0]
    row_ref[0] = wave_ref[...]
    row_ref[1], row_ref[2] = turn(wave_ref[...] * 128.0, *constants(blocks))
    points, inverse, quarter = constants(TROWS)
    lane = lax.broadcasted_iota(jnp.int32, (TROWS, 128), 1).astype(F32)

    def columns(i, col_ref):
        for k in range(3):
            col_ref[k] = jnp.broadcast_to(row_ref[k, pl.ds(i, 1), :], (128, 128)).T

    def fill(i, col_ref):
        for t in range(128 // TROWS):
            at = pl.ds(pl.multiple_of(i * 128 + t * TROWS, TROWS), TROWS)
            wave, step_cos, step_sin = (col_ref[k, t * TROWS : (t + 1) * TROWS, :] for k in range(3))
            cos, sin = turn(wave * lane, points, inverse, quarter)
            twice = 2.0 * step_cos
            last = cos * step_cos + sin * step_sin, sin * step_cos - cos * step_sin
            for u in range(QPAD // 128):
                cos_ref[at, 128 * u : 128 * u + 128] = cos.astype(BF16)
                sin_ref[at, 128 * u : 128 * u + 128] = sin.astype(BF16)
                following = twice * cos - last[0], twice * sin - last[1]
                last = cos, sin
                cos, sin = following

    columns(0, even_ref)

    def pair(p, carry):
        columns(2 * p + 1, odd_ref)
        fill(2 * p, even_ref)
        columns(jnp.minimum(2 * p + 2, blocks - 1), even_ref)
        fill(2 * p + 1, odd_ref)
        return carry

    lax.fori_loop(0, blocks // 2, pair, 0)


def trig_tables(points, wave_rows):
    vmem = pl.BlockSpec(memory_space=pltpu.VMEM)
    shape = jax.ShapeDtypeStruct((KPAD, QPAD), BF16)
    return pl.pallas_call(
        table_kernel,
        in_specs=[pl.BlockSpec(memory_space=pltpu.SMEM), vmem],
        out_specs=[vmem, vmem],
        out_shape=[shape, shape],
        scratch_shapes=[
            pltpu.VMEM((3,) + wave_rows.shape, F32),
            pltpu.VMEM((3, 128, 128), F32),
            pltpu.VMEM((3, 128, 128), F32),
        ],
        compiler_params=pltpu.CompilerParams(vmem_limit_bytes=8 << 20),
        name="tables",
    )(points, wave_rows)


def coefficients(message):
    turned = message.astype(F32).T
    real = jnp.concatenate([turned[32 * k : 32 * k + 16] for k in range(GROUP)], axis=1)
    imag = jnp.concatenate([turned[32 * k + 16 : 32 * k + 32] for k in range(GROUP)], axis=1)
    return real, imag


def classes(wave, points_int, scale):
    valid = (wave < M) & (2 * wave < points_int)
    kind = wave & 3
    return [jnp.where(valid & (kind == k), scale, 0.0) for k in range(4)]


def inverse_quarters(real, imag, wave, points_int, cos_ref, sin_ref):
    doubled = jnp.where(wave == 0, 1.0, 2.0)
    e0, e1, e2, e3 = classes(wave, points_int, doubled)
    odd = e1 + e3
    turned = e1 - e3
    left_cos = jnp.concatenate([real * e0, real * e2, real * odd, imag * turned], axis=0).astype(BF16)
    left_sin = jnp.concatenate([imag * -e0, imag * -e2, imag * -odd, real * turned], axis=0).astype(BF16)
    sums = jnp.dot(left_cos, cos_ref[...], preferred_element_type=F32)
    sums += jnp.dot(left_sin, sin_ref[...], preferred_element_type=F32)
    even = sums[0:16] + sums[16:32]
    odds = sums[0:16] - sums[16:32]
    return even + sums[32:48], odds - sums[48:64], even - sums[32:48], odds + sums[48:64]


def grid_kernel(points_ref, wave_ref, own_ref, cos_ref, sin_ref, out_ref, line_ref):
    points_int = points_ref[0]
    quarter = points_int >> 2
    real, imag = coefficients(own_ref[...])
    quarters = inverse_quarters(real, imag, wave_ref[...], points_int, cos_ref, sin_ref)
    line_ref[...] = jnp.zeros_like(line_ref)
    keep = lax.broadcasted_iota(jnp.int32, (16, QPAD), 1) < quarter
    for t in range(4):
        part = jnp.where(keep, quarters[t], 0.0)
        part = jnp.concatenate([part, jnp.zeros((16, 128), F32)], axis=1)
        if t == 0:
            line_ref[:, : QPAD + 128] += part
        else:
            first = quarter * t
            part = pltpu.roll(part, first & 127, 1)
            at = pl.ds(pl.multiple_of((first >> 7) * 128, 128), QPAD + 128)
            line_ref[:, at] += part
    bands, _, width = out_ref.shape
    for k in range(bands):
        out_ref[k] = line_ref[:, k * width : (k + 1) * width].astype(BF16)


def grid_rows(points, wave, own, cos, sin, bands):
    vmem = pl.BlockSpec(memory_space=pltpu.VMEM)
    return pl.pallas_call(
        grid_kernel,
        in_specs=[pl.BlockSpec(memory_space=pltpu.SMEM)] + [vmem] * 4,
        out_specs=vmem,
        out_shape=jax.ShapeDtypeStruct((bands, 16, LONS // bands), BF16),
        scratch_shapes=[pltpu.VMEM((16, LONS), F32)],
        compiler_params=pltpu.CompilerParams(vmem_limit_bytes=16 << 20),
        name="grid",
    )(points, wave, own, cos, sin)


def gather_kernel(rows_ref, out_ref):
    fields = rows_ref.shape[1]
    for k in range(rows_ref.shape[0]):
        out_ref[k * fields : (k + 1) * fields, 0, :] = rows_ref[k].astype(F32)


def gather_rows(rows):
    bands, fields, width = rows.shape
    vmem = pl.BlockSpec(memory_space=pltpu.VMEM)
    return pl.pallas_call(
        gather_kernel,
        in_specs=[vmem],
        out_specs=vmem,
        out_shape=jax.ShapeDtypeStruct((bands * fields, 1, width), F32),
        compiler_params=pltpu.CompilerParams(vmem_limit_bytes=4 << 20),
        name="gather",
    )(rows)


def scale_quarters(quarter, scale_ref, line_ref):
    bands = scale_ref.shape[0]
    tiles = LONS // (128 * bands)
    for k in range(bands):
        for i in range(tiles):
            at = 128 * (k * tiles + i)
            line_ref[:, at : at + 128] = jnp.broadcast_to(scale_ref[k, i : i + 1, :], (8, 128))
    keep = lax.broadcasted_iota(jnp.int32, (8, QPAD), 1) < quarter
    wide = QPAD + 128
    parts = []
    for t in range(4):
        first = quarter * t
        part = line_ref[:, pl.ds(pl.multiple_of((first >> 7) * 128, 128), wide)]
        part = pltpu.roll(part, lax.rem(wide - (first & 127), wide), 1)
        parts.append(jnp.where(keep, part[:, :QPAD], 0.0)[0:1])
    return parts


def back_kernel(
    points_ref, band_ref, wave_ref, own_ref, other_ref, mix_ref, scale_ref, cos_ref, sin_ref, out_ref, line_ref
):
    points_int = points_ref[0]
    quarter = points_int >> 2
    low = (band_ref[0] & 1) == 0
    wave = wave_ref[...]
    own = coefficients(own_ref[...])
    other = coefficients(other_ref[...])
    mix = jnp.where(low, mix_ref[0:16, :], mix_ref[16:32, :])
    high = mix.astype(BF16)
    rest = mix - high.astype(F32)
    middle = rest.astype(BF16)
    last = (rest - middle.astype(F32)).astype(BF16)
    factors = jnp.concatenate([high.astype(F32), middle.astype(F32), last.astype(F32)], axis=0).astype(BF16)
    mixed = []
    for mine, its in zip(own, other):
        levels = jnp.concatenate([jnp.where(low, mine, its), jnp.where(low, its, mine)], axis=0).astype(BF16)
        terms = jnp.dot(factors, levels, preferred_element_type=F32)
        mixed.append(terms[0:16] + terms[16:32] + terms[32:48])
    quarters = inverse_quarters(mixed[0], mixed[1], wave, points_int, cos_ref, sin_ref)
    scales = scale_quarters(quarter, scale_ref, line_ref)
    q0, q1, q2, q3 = (part * scale for part, scale in zip(quarters, scales))
    even = q0 + q2
    odds = q1 + q3
    folded = jnp.concatenate([even + odds, even - odds, q0 - q2, q1 - q3], axis=0).astype(BF16)
    by_cos = lax.dot_general(folded, cos_ref[...], NT, preferred_element_type=F32)
    by_sin = lax.dot_general(folded, sin_ref[...], NT, preferred_element_type=F32)
    inverse = 1.0 / jnp.full((1, KPAD), points_int, jnp.int32).astype(F32)
    v0, v1, v2, v3 = classes(wave, points_int, inverse)
    odd = v1 + v3
    cosines = by_cos[0:16] * v0 + by_cos[16:32] * v2 + by_cos[32:48] * odd + by_sin[48:64] * (v3 - v1)
    sines = by_sin[0:16] * v0 + by_sin[16:32] * v2 + by_sin[32:48] * odd + by_cos[48:64] * (v1 - v3)
    width = LAT * ROWS
    rows = []
    for k in range(GROUP):
        rows.append(cosines[:, k * width : (k + 1) * width])
        rows.append(-sines[:, k * width : (k + 1) * width])
    rows.append(jnp.zeros((128 - 32 * GROUP, width), F32))
    out_ref[...] = jnp.concatenate(rows, axis=0).T.astype(BF16)


def back_rows(points, band, wave, own, other, mix, scale, cos, sin):
    vmem = pl.BlockSpec(memory_space=pltpu.VMEM)
    smem = pl.BlockSpec(memory_space=pltpu.SMEM)
    return pl.pallas_call(
        back_kernel,
        in_specs=[smem, smem] + [vmem] * 7,
        out_specs=vmem,
        out_shape=jax.ShapeDtypeStruct((LAT * ROWS, 128), BF16),
        scratch_shapes=[pltpu.VMEM((8, LONS), F32)],
        compiler_params=pltpu.CompilerParams(vmem_limit_bytes=16 << 20),
        name="back",
    )(points, band, wave, own, other, mix, scale, cos, sin)


def body(spectral, legendre, slot_wave, lat_points, level_mix, grid_scale, gauss_w):
    slots = spectral.shape[0]
    bands = lax.axis_size("band")
    base = (lax.axis_index("wave") * slots).astype(jnp.int32)[None]
    band = lax.axis_index("band").astype(jnp.int32)[None]

    width = grid_scale.shape[1]

    scale = jnp.pad(grid_scale.reshape(1, width // 128, 128), ((0, 0), (0, 8 - width // 128), (0, 0)))
    scale = lax.all_to_all(jnp.broadcast_to(scale, (bands, 8, 128)), "band", 0, 0, tiled=True)
    four = legendre_inverse(base, slot_wave, spectral, legendre)

    by_row = jnp.pad(slot_wave.reshape(LAT, ROWS - 1, GROUP), ((0, 0), (0, 1), (0, 0)), constant_values=M)
    wave = jnp.transpose(by_row, (2, 0, 1)).reshape(1, KPAD)
    wave_rows = wave.reshape(KPAD // 128, 128).astype(F32)

    four, scale, wave, wave_rows, band = lax.optimization_barrier((four, scale, wave, wave_rows, band))
    message = lax.all_to_all(four.reshape(LAT, ROWS, 128), "wave", 0, 0, tiled=True)
    own, points = lax.optimization_barrier((message.reshape(LAT * ROWS, 128), lat_points))
    other = lax.ppermute(own, "band", [(k, k ^ 1) for k in range(bands)])
    cos, sin = trig_tables(points, wave_rows)
    rows = grid_rows(points, wave, own, cos, sin, bands)
    back = back_rows(points, band, wave, own, other, level_mix, scale, cos, sin)
    back = lax.all_to_all(back.reshape(LAT, ROWS, 128), "wave", 0, 0, tiled=True)
    rows, back = lax.optimization_barrier((rows, back))
    rows = lax.all_to_all(rows, "band", 0, 0, tiled=True)
    spec_out = legendre_direct(base, slot_wave, back.reshape(LAT * ROWS, 128), legendre, gauss_w)
    return gather_rows(rows), spec_out.reshape(spectral.shape)


def solution(mesh):
    placed = (
        P("wave", None, "band", None),
        P("wave", None, None),
        P(),
        P("wave"),
        P(),
        P("wave", "band"),
        P(),
    )

    return jax.shard_map(
        body,
        mesh=mesh,
        in_specs=placed,
        out_specs=(P(None, "wave", "band"), P("wave", None, "band", None)),
        check_vma=False,
    )
```

```python
import math

import jax
import jax.numpy as jnp
from jax import lax
from jax.experimental import pallas as pl
from jax.experimental.pallas import tpu as pltpu
from jax.sharding import PartitionSpec as P


M = 1280
LAT = 96
GROUP = 3
ROWS = 8
KPAD = GROUP * LAT * ROWS
QPAD = 1408
LONS = 6144
TWO_PI = 2.0 * math.pi
F32 = jnp.float32
BF16 = jnp.bfloat16

NT = (((1,), (1,)), ((), ()))


def spectral_copies(spec_ref, leg_ref, spec_buf, leg_buf, sems):
    copies = []
    for step in range(leg_ref.shape[0] // GROUP):
        at = pl.ds(step * GROUP, GROUP)
        copies.append(
            (
                pltpu.make_async_copy(spec_ref.at[at], spec_buf.at[at], sems.at[0, step]),
                pltpu.make_async_copy(leg_ref.at[at], leg_buf.at[at], sems.at[1, step]),
            )
        )
    return copies


def legendre_inverse_kernel(base_ref, wave_ref, spec_ref, leg_ref, out_ref, spec_buf, leg_buf, acc_ref, sems):
    copies = spectral_copies(spec_ref, leg_ref, spec_buf, leg_buf, sems)
    for pair in copies:
        for copy in pair:
            copy.start()
    acc_ref[pl.ds(ROWS - 1, LAT, stride=ROWS), :] = jnp.zeros((LAT, 128), F32)
    degree = lax.broadcasted_iota(jnp.int32, (32, M), 1)
    for step, pair in enumerate(copies):
        for copy in pair:
            copy.wait()
        parts = []
        for k in range(step * GROUP, step * GROUP + GROUP):
            wave = wave_ref[base_ref[0] + k]
            coef = jnp.where(degree >= wave, spec_buf[k].astype(F32), 0.0).astype(BF16)
            parts.append(lax.dot_general(leg_buf[k], coef, NT, preferred_element_type=F32))
        parts.append(jnp.zeros((LAT, 32), F32))
        acc_ref[pl.ds(step, LAT, stride=ROWS), :] = jnp.concatenate(parts, axis=1)
    out_ref[...] = acc_ref[...].astype(BF16)


def legendre_inverse(base, slot_wave, spectral, legendre):
    slots = spectral.shape[0]
    smem = pl.BlockSpec(memory_space=pltpu.SMEM)
    hbm = pl.BlockSpec(memory_space=pl.ANY)
    return pl.pallas_call(
        legendre_inverse_kernel,
        in_specs=[smem, smem, hbm, hbm],
        out_specs=pl.BlockSpec(memory_space=pltpu.VMEM),
        out_shape=jax.ShapeDtypeStruct((LAT * ROWS, 128), BF16),
        scratch_shapes=[
            pltpu.VMEM((slots, 32, M), BF16),
            pltpu.VMEM((slots, LAT, M), BF16),
            pltpu.VMEM((LAT * ROWS, 128), F32),
            pltpu.SemaphoreType.DMA((2, slots // GROUP)),
        ],
        name="legendre_inverse",
    )(base, slot_wave, spectral.reshape(slots, 32, M), legendre)


def legendre_direct_kernel(base_ref, wave_ref, coef_ref, leg_ref, gauss_ref, out_ref, leg_buf, out_buf, acc_ref, sems):
    steps = leg_ref.shape[0] // GROUP
    loads = []
    stores = []
    for step in range(steps):
        at = pl.ds(step * GROUP, GROUP)
        loads.append(pltpu.make_async_copy(leg_ref.at[at], leg_buf.at[at], sems.at[0, step]))
        stores.append(pltpu.make_async_copy(out_buf.at[at], out_ref.at[at], sems.at[1, step]))
    for copy in loads:
        copy.start()
    acc_ref[pl.ds(0, LAT * ROWS), :] = coef_ref[...].astype(F32)
    acc_ref[pl.ds(LAT * ROWS, (128 - LAT) * ROWS), :] = jnp.zeros(((128 - LAT) * ROWS, 128), F32)
    degree = lax.broadcasted_iota(jnp.int32, (32, M), 1)
    for step in range(steps):
        rows = acc_ref[pl.ds(step, 128, stride=ROWS), :]
        weighted = (rows.T[:, :LAT] * gauss_ref[...]).astype(BF16)
        loads[step].wait()
        for j in range(GROUP):
            k = step * GROUP + j
            wave = wave_ref[base_ref[0] + k]
            summed = jnp.dot(weighted[32 * j : 32 * j + 32], leg_buf[k], preferred_element_type=F32)
            out_buf[k] = jnp.where(degree >= wave, summed, 0.0).astype(BF16)
        stores[step].start()
    for copy in stores:
        copy.wait()


def legendre_direct(base, slot_wave, coef, legendre, gauss_w):
    slots = legendre.shape[0]
    smem = pl.BlockSpec(memory_space=pltpu.SMEM)
    vmem = pl.BlockSpec(memory_space=pltpu.VMEM)
    hbm = pl.BlockSpec(memory_space=pl.ANY)
    return pl.pallas_call(
        legendre_direct_kernel,
        in_specs=[smem, smem, vmem, hbm, vmem],
        out_specs=hbm,
        out_shape=jax.ShapeDtypeStruct((slots, 32, M), BF16),
        scratch_shapes=[
            pltpu.VMEM((slots, LAT, M), BF16),
            pltpu.VMEM((slots, 32, M), BF16),
            pltpu.VMEM((128 * ROWS, 128), F32),
            pltpu.SemaphoreType.DMA((2, slots // GROUP)),
        ],
        name="legendre_direct",
    )(base, slot_wave, coef, legendre, gauss_w[None, :])


def turn(product, points, inverse, quarter):
    rest = product - jnp.floor(product * inverse) * points
    rest = jnp.where(rest < 0.0, rest + points, rest)
    rest = jnp.where(rest >= points, rest - points, rest)
    quad = jnp.floor(rest * (4.0 * inverse) + 0.5)
    x = (rest - quad * quarter) * (TWO_PI * inverse)
    x2 = x * x
    s = x + x * x2 * (-1.6666654611e-1 + x2 * (8.3321608736e-3 - x2 * 1.9515295891e-4))
    c = 1.0 - 0.5 * x2 + x2 * x2 * (
        4.166664568298827e-2 + x2 * (-1.388731625493765e-3 + x2 * 2.443315711809948e-5)
    )
    swap = (quad == 1.0) | (quad == 3.0)
    cos = jnp.where(swap, s, c)
    sin = jnp.where(swap, c, s)
    cos = jnp.where((quad == 1.0) | (quad == 2.0), -cos, cos)
    sin = jnp.where((quad == 2.0) | (quad == 3.0), -sin, sin)
    return cos, sin


TROWS = 32


def table_kernel(points_ref, wave_ref, cos_ref, sin_ref, row_ref, even_ref, odd_ref):
    points_int = points_ref[0]

    def constants(rows):
        points = jnp.full((rows, 128), points_int, jnp.int32).astype(F32)
        quarter = jnp.full((rows, 128), points_int >> 2, jnp.int32).astype(F32)
        return points, 1.0 / points, quarter

    blocks = wave_ref.shape[0]
    row_ref[0] = wave_ref[...]
    row_ref[1], row_ref[2] = turn(wave_ref[...] * 128.0, *constants(blocks))
    points, inverse, quarter = constants(TROWS)
    lane = lax.broadcasted_iota(jnp.int32, (TROWS, 128), 1).astype(F32)

    def columns(i, col_ref):
        for k in range(3):
            col_ref[k] = jnp.broadcast_to(row_ref[k, pl.ds(i, 1), :], (128, 128)).T

    def fill(i, col_ref):
        for t in range(128 // TROWS):
            at = pl.ds(pl.multiple_of(i * 128 + t * TROWS, TROWS), TROWS)
            wave, step_cos, step_sin = (col_ref[k, t * TROWS : (t + 1) * TROWS, :] for k in range(3))
            cos, sin = turn(wave * lane, points, inverse, quarter)
            twice = 2.0 * step_cos
            last = cos * step_cos + sin * step_sin, sin * step_cos - cos * step_sin
            for u in range(QPAD // 128):
                cos_ref[at, 128 * u : 128 * u + 128] = cos.astype(BF16)
                sin_ref[at, 128 * u : 128 * u + 128] = sin.astype(BF16)
                following = twice * cos - last[0], twice * sin - last[1]
                last = cos, sin
                cos, sin = following

    columns(0, even_ref)

    def pair(p, carry):
        columns(2 * p + 1, odd_ref)
        fill(2 * p, even_ref)
        columns(jnp.minimum(2 * p + 2, blocks - 1), even_ref)
        fill(2 * p + 1, odd_ref)
        return carry

    lax.fori_loop(0, blocks // 2, pair, 0)


def trig_tables(points, wave_rows):
    vmem = pl.BlockSpec(memory_space=pltpu.VMEM)
    shape = jax.ShapeDtypeStruct((KPAD, QPAD), BF16)
    return pl.pallas_call(
        table_kernel,
        in_specs=[pl.BlockSpec(memory_space=pltpu.SMEM), vmem],
        out_specs=[vmem, vmem],
        out_shape=[shape, shape],
        scratch_shapes=[
            pltpu.VMEM((3,) + wave_rows.shape, F32),
            pltpu.VMEM((3, 128, 128), F32),
            pltpu.VMEM((3, 128, 128), F32),
        ],
        compiler_params=pltpu.CompilerParams(vmem_limit_bytes=8 << 20),
        name="tables",
    )(points, wave_rows)


def coefficients(message):
    turned = message.astype(F32).T
    real = jnp.concatenate([turned[32 * k : 32 * k + 16] for k in range(GROUP)], axis=1)
    imag = jnp.concatenate([turned[32 * k + 16 : 32 * k + 32] for k in range(GROUP)], axis=1)
    return real, imag


def classes(wave, points_int, scale):
    valid = (wave < M) & (2 * wave < points_int)
    kind = wave & 3
    return [jnp.where(valid & (kind == k), scale, 0.0) for k in range(4)]


def inverse_quarters(real, imag, wave, points_int, cos_ref, sin_ref):
    doubled = jnp.where(wave == 0, 1.0, 2.0)
    e0, e1, e2, e3 = classes(wave, points_int, doubled)
    odd = e1 + e3
    turned = e1 - e3
    left_cos = jnp.concatenate([real * e0, real * e2, real * odd, imag * turned], axis=0).astype(BF16)
    left_sin = jnp.concatenate([imag * -e0, imag * -e2, imag * -odd, real * turned], axis=0).astype(BF16)
    sums = jnp.dot(left_cos, cos_ref[...], preferred_element_type=F32)
    sums += jnp.dot(left_sin, sin_ref[...], preferred_element_type=F32)
    even = sums[0:16] + sums[16:32]
    odds = sums[0:16] - sums[16:32]
    return even + sums[32:48], odds - sums[48:64], even - sums[32:48], odds + sums[48:64]


def grid_kernel(points_ref, wave_ref, own_ref, cos_ref, sin_ref, out_ref, line_ref):
    points_int = points_ref[0]
    quarter = points_int >> 2
    real, imag = coefficients(own_ref[...])
    quarters = inverse_quarters(real, imag, wave_ref[...], points_int, cos_ref, sin_ref)
    line_ref[...] = jnp.zeros_like(line_ref)
    keep = lax.broadcasted_iota(jnp.int32, (16, QPAD), 1) < quarter
    for t in range(4):
        part = jnp.where(keep, quarters[t], 0.0)
        part = jnp.concatenate([part, jnp.zeros((16, 128), F32)], axis=1)
        if t == 0:
            line_ref[:, : QPAD + 128] += part
        else:
            first = quarter * t
            part = pltpu.roll(part, first & 127, 1)
            at = pl.ds(pl.multiple_of((first >> 7) * 128, 128), QPAD + 128)
            line_ref[:, at] += part
    bands, _, width = out_ref.shape
    for k in range(bands):
        out_ref[k] = line_ref[:, k * width : (k + 1) * width].astype(BF16)


def grid_rows(points, wave, own, cos, sin, bands):
    vmem = pl.BlockSpec(memory_space=pltpu.VMEM)
    return pl.pallas_call(
        grid_kernel,
        in_specs=[pl.BlockSpec(memory_space=pltpu.SMEM)] + [vmem] * 4,
        out_specs=vmem,
        out_shape=jax.ShapeDtypeStruct((bands, 16, LONS // bands), BF16),
        scratch_shapes=[pltpu.VMEM((16, LONS), F32)],
        compiler_params=pltpu.CompilerParams(vmem_limit_bytes=16 << 20),
        name="grid",
    )(points, wave, own, cos, sin)


def gather_kernel(rows_ref, out_ref):
    fields = rows_ref.shape[1]
    for k in range(rows_ref.shape[0]):
        out_ref[k * fields : (k + 1) * fields, 0, :] = rows_ref[k].astype(F32)


def gather_rows(rows):
    bands, fields, width = rows.shape
    vmem = pl.BlockSpec(memory_space=pltpu.VMEM)
    return pl.pallas_call(
        gather_kernel,
        in_specs=[vmem],
        out_specs=vmem,
        out_shape=jax.ShapeDtypeStruct((bands * fields, 1, width), F32),
        compiler_params=pltpu.CompilerParams(vmem_limit_bytes=4 << 20),
        name="gather",
    )(rows)


def scale_quarters(band, quarter, scale_ref, line_ref):
    bands, width = scale_ref.shape
    for k in range(bands):
        row = scale_ref[pl.ds(band ^ k, 1), :]
        line_ref[:, k * width : (k + 1) * width] = jnp.broadcast_to(row, (8, width))
    keep = lax.broadcasted_iota(jnp.int32, (8, QPAD), 1) < quarter
    wide = QPAD + 128
    parts = []
    for t in range(4):
        first = quarter * t
        part = line_ref[:, pl.ds(pl.multiple_of((first >> 7) * 128, 128), wide)]
        part = pltpu.roll(part, lax.rem(wide - (first & 127), wide), 1)
        parts.append(jnp.where(keep, part[:, :QPAD], 0.0)[0:1])
    return parts


def back_kernel(
    points_ref, band_ref, wave_ref, own_ref, other_ref, mix_ref, scale_ref, cos_ref, sin_ref, out_ref, line_ref
):
    points_int = points_ref[0]
    quarter = points_int >> 2
    low = (band_ref[0] & 1) == 0
    wave = wave_ref[...]
    own = coefficients(own_ref[...])
    other = coefficients(other_ref[...])
    mix = jnp.where(low, mix_ref[0:16, :], mix_ref[16:32, :])
    high = mix.astype(BF16)
    rest = mix - high.astype(F32)
    middle = rest.astype(BF16)
    last = (rest - middle.astype(F32)).astype(BF16)
    factors = jnp.concatenate([high.astype(F32), middle.astype(F32), last.astype(F32)], axis=0).astype(BF16)
    mixed = []
    for mine, its in zip(own, other):
        levels = jnp.concatenate([jnp.where(low, mine, its), jnp.where(low, its, mine)], axis=0).astype(BF16)
        terms = jnp.dot(factors, levels, preferred_element_type=F32)
        mixed.append(terms[0:16] + terms[16:32] + terms[32:48])
    quarters = inverse_quarters(mixed[0], mixed[1], wave, points_int, cos_ref, sin_ref)
    scales = scale_quarters(band_ref[0], quarter, scale_ref, line_ref)
    q0, q1, q2, q3 = (part * scale for part, scale in zip(quarters, scales))
    even = q0 + q2
    odds = q1 + q3
    folded = jnp.concatenate([even + odds, even - odds, q0 - q2, q1 - q3], axis=0).astype(BF16)
    by_cos = lax.dot_general(folded, cos_ref[...], NT, preferred_element_type=F32)
    by_sin = lax.dot_general(folded, sin_ref[...], NT, preferred_element_type=F32)
    inverse = 1.0 / jnp.full((1, KPAD), points_int, jnp.int32).astype(F32)
    v0, v1, v2, v3 = classes(wave, points_int, inverse)
    odd = v1 + v3
    cosines = by_cos[0:16] * v0 + by_cos[16:32] * v2 + by_cos[32:48] * odd + by_sin[48:64] * (v3 - v1)
    sines = by_sin[0:16] * v0 + by_sin[16:32] * v2 + by_sin[32:48] * odd + by_cos[48:64] * (v1 - v3)
    width = LAT * ROWS
    rows = []
    for k in range(GROUP):
        rows.append(cosines[:, k * width : (k + 1) * width])
        rows.append(-sines[:, k * width : (k + 1) * width])
    rows.append(jnp.zeros((128 - 32 * GROUP, width), F32))
    out_ref[...] = jnp.concatenate(rows, axis=0).T.astype(BF16)


def back_rows(points, band, wave, own, other, mix, scale, cos, sin):
    vmem = pl.BlockSpec(memory_space=pltpu.VMEM)
    smem = pl.BlockSpec(memory_space=pltpu.SMEM)
    return pl.pallas_call(
        back_kernel,
        in_specs=[smem, smem] + [vmem] * 7,
        out_specs=vmem,
        out_shape=jax.ShapeDtypeStruct((LAT * ROWS, 128), BF16),
        scratch_shapes=[pltpu.VMEM((8, LONS), F32)],
        compiler_params=pltpu.CompilerParams(vmem_limit_bytes=16 << 20),
        name="back",
    )(points, band, wave, own, other, mix, scale, cos, sin)


def body(spectral, legendre, slot_wave, lat_points, level_mix, grid_scale, gauss_w):
    slots = spectral.shape[0]
    bands = lax.axis_size("band")
    base = (lax.axis_index("wave") * slots).astype(jnp.int32)[None]
    band = lax.axis_index("band").astype(jnp.int32)[None]


    def swap(array, k):
        return lax.ppermute(array, "band", [(i, i ^ k) for i in range(bands)])

    four = legendre_inverse(base, slot_wave, spectral, legendre)
    message = lax.all_to_all(four.reshape(LAT, ROWS, 128), "wave", 0, 0, tiled=True)

    scale = grid_scale
    for k in (1, 2, 4):
        scale = jnp.concatenate([scale, swap(scale, k)], axis=0)

    by_row = jnp.pad(slot_wave.reshape(LAT, ROWS - 1, GROUP), ((0, 0), (0, 1), (0, 0)), constant_values=M)
    wave = jnp.transpose(by_row, (2, 0, 1)).reshape(1, KPAD)
    wave_rows = wave.reshape(KPAD // 128, 128).astype(F32)

    own, scale, wave, wave_rows, points, band = lax.optimization_barrier(
        (message.reshape(LAT * ROWS, 128), scale, wave, wave_rows, lat_points, band)
    )
    other = swap(own, 1)
    cos, sin = trig_tables(points, wave_rows)
    rows = grid_rows(points, wave, own, cos, sin, bands)
    back = back_rows(points, band, wave, own, other, level_mix, scale, cos, sin)
    back = lax.all_to_all(back.reshape(LAT, ROWS, 128), "wave", 0, 0, tiled=True)
    rows, back = lax.optimization_barrier((rows, back))
    rows = lax.all_to_all(rows, "band", 0, 0, tiled=True)
    spec_out = legendre_direct(base, slot_wave, back.reshape(LAT * ROWS, 128), legendre, gauss_w)
    return gather_rows(rows), spec_out.reshape(spectral.shape)


def solution(mesh):
    placed = (
        P("wave", None, "band", None),
        P("wave", None, None),
        P(),
        P("wave"),
        P(),
        P("wave", "band"),
        P(),
    )

    return jax.shard_map(
        body,
        mesh=mesh,
        in_specs=placed,
        out_specs=(P(None, "wave", "band"), P("wave", None, "band", None)),
        check_vma=False,
    )
```
